256 devices in a mesh: freq: 16 (over z, core), bl: 16 (over y, x).
Axes of the slice: x: 4, y: 4, z: 8, core: 2. Of those that a mesh axis runs over, the one named last changes fastest.
Arguments:
- visibilities: float32 [2, 64, 4, 131072], P(None, 'freq', None, 'bl')
- sky_model: bfloat16 [2, 64, 8, 4, 131072], P(None, 'freq', None, None, 'bl')
- flag_mask: int32 [4, 131072], P(None, 'bl'), may hold values from 0 to 1
- first_station: int32 [131072], P('bl'), may hold values from 0 to 511
- second_station: int32 [131072], P('bl'), may hold values from 0 to 511, as said below
- gain_start: float32 [2, 64, 8, 512], P(None, 'freq')
- dual_start: float32 [2, 64, 8, 512], P(None, 'freq'), may hold values from -1.8 to 1.8
- consensus_start: float32 [3, 2, 8, 512], replicated, may hold values from -27.495455 to 27.495455
- penalty: float32 [8], replicated, may hold values from 0.3 to 3
Outputs:
- gain_final: float32 [2, 64, 8, 512], P(None, 'freq')
- dual_final: float32 [2, 64, 8, 512], P(None, 'freq')
- consensus_final: float32 [3, 2, 8, 512], replicated
The draws below stay inside these ranges and needn't reach their ends.
Inputs may be any that keep to these rules, and one draw needn't show every extreme that they name: `second_station`: differs from first_station on every baseline.
All inputs are finite; a program needn't handle non-finite values.
Results may differ from the reference program's by a relative error of at most 0.0003.
Values sent between devices are 32-bit elements; how exact they have to be, the bound alone decides.
No kernel may reach another device: no remote copies, remote signals or barrier semaphores. Data moves between devices by JAX's collectives and lax.ppermute only.
A program may use at most 64 MiB of HBM per device.

```python
import math
import jax
import jax.numpy as jnp
from jax import lax

P_SIZE = 512
KDIR = 8
TS = 4
NPOLY = 3
NIT = 3
BL_DEV = 8192
CH = 64
NBL = 131072


def station_pairs(key):
    pair_key = jax.random.fold_in(key, 11)
    first_key, second_key = jax.random.split(pair_key)
    first_ids = jax.random.randint(first_key, (NBL,), 0, P_SIZE, dtype=jnp.int32)
    step_ids = jax.random.randint(second_key, (NBL,), 1, P_SIZE, dtype=jnp.int32)
    return (first_ids, (first_ids + step_ids) % P_SIZE)


def true_gains(key):
    gain_key = jax.random.fold_in(key, 12)
    amplitude_key, phase_key = jax.random.split(gain_key)
    amplitude = jax.random.uniform(amplitude_key, (CH, KDIR, P_SIZE), jnp.float32, 0.7, 1.3)
    phase_values = jax.random.uniform(phase_key, (CH, KDIR, P_SIZE), jnp.float32, -math.pi, math.pi)
    return jnp.stack([amplitude * jnp.cos(phase_values), amplitude * jnp.sin(phase_values)])


def sky_scale():
    return math.sqrt(P_SIZE / (NBL * TS))


def sky_field(key):
    sky_key = jax.random.fold_in(key, 13)
    values = sky_scale() * jax.random.normal(sky_key, (2, CH, KDIR, TS, NBL), jnp.float32)
    return values.astype(jnp.bfloat16)


def draw_sky_model(key, part):
    return sky_field(key)


def draw_first_station(key, part):
    return station_pairs(key)[0]


def draw_second_station(key, part):
    return station_pairs(key)[1]


def draw_gain_start(key, part):
    noise_values = 0.3 * jax.random.normal(jax.random.fold_in(key, 15), (2, CH, KDIR, P_SIZE), jnp.float32)
    return true_gains(key) + noise_values


def draw_flag_mask(key, part):
    mask_key = jax.random.fold_in(key, 14)
    left_key, right_key, element_key = jax.random.split(mask_key, 3)
    block_length = math.gcd(BL_DEV, 512)
    count_of_blocks = NBL // block_length
    block_level = 1 + jax.random.randint(left_key, (count_of_blocks,), 0, 4, dtype=jnp.int32) * jax.random.randint(right_key, (count_of_blocks,), 0, 4, dtype=jnp.int32)
    level_row_table = jnp.repeat(block_level, block_length)
    random_element_samples = jax.random.randint(element_key, (TS, NBL), 0, 10, dtype=jnp.int32)
    return (random_element_samples < level_row_table[None, :]).astype(jnp.int32)


def draw_visibilities(key, part):
    first_ids, second_station_index = station_pairs(key)
    true_values = true_gains(key)
    sky_values = sky_field(key).astype(jnp.float32)
    total_real = jnp.zeros((CH, TS, NBL), jnp.float32)
    total_imag = jnp.zeros((CH, TS, NBL), jnp.float32)
    for direction in range(KDIR):
        first_gain = true_values[:, :, direction][:, :, first_ids][:, :, None, :]
        second_gain = true_values[:, :, direction][:, :, second_station_index][:, :, None, :]
        sky_real = sky_values[0, :, direction]
        sky_imag = sky_values[1, :, direction]
        apparent_real = sky_real * second_gain[0] + sky_imag * second_gain[1]
        apparent_imag = sky_imag * second_gain[0] - sky_real * second_gain[1]
        total_real = total_real + first_gain[0] * apparent_real - first_gain[1] * apparent_imag
        total_imag = total_imag + first_gain[0] * apparent_imag + first_gain[1] * apparent_real
    noise_values = 0.1 * math.sqrt(KDIR) * sky_scale() * jax.random.normal(jax.random.fold_in(key, 16), (2, CH, TS, NBL), jnp.float32)
    return jnp.stack([total_real, total_imag]) + noise_values


def levels(key, dims, pieces, low, high):
    def one(axis_at, parts):
        steps = jax.random.uniform(jax.random.fold_in(jax.random.fold_in(key, 6), axis_at), (parts,), jnp.float32, low / len(pieces), high / len(pieces))
        return jnp.repeat(jnp.exp(steps), dims[axis_at] // parts).reshape((-1,) + (1,) * (len(dims) - axis_at - 1))

    factor_of = one(*pieces[0])
    for cut in pieces[1:]:
        factor_of = factor_of * one(*cut)
    return factor_of


def gaussian(own_key, shape, width, bound, pieces=(), kind=jnp.bfloat16):
    loudness = levels(own_key, shape, pieces, -0.22, 0.18) if pieces else 1.0
    drawn = jax.random.normal(own_key, shape, jnp.float32) * width * loudness
    return jnp.minimum(jnp.maximum(drawn, -bound), bound).astype(kind)


def setup_inputs(seed: int = 0) -> dict:
    key_of = jax.random.split(jax.random.key(seed), 10)
    return {
        "visibilities": draw_visibilities(jax.random.fold_in(key_of[9], 71), 0),
        "sky_model": draw_sky_model(jax.random.fold_in(key_of[9], 71), 0),
        "flag_mask": draw_flag_mask(jax.random.fold_in(key_of[9], 71), 0),
        "first_station": draw_first_station(jax.random.fold_in(key_of[9], 71), 0),
        "second_station": draw_second_station(jax.random.fold_in(key_of[9], 71), 0),
        "gain_start": draw_gain_start(jax.random.fold_in(key_of[9], 71), 0),
        "dual_start": gaussian(key_of[6], (2, CH, KDIR, P_SIZE), 0.3, 1.8, ((1, 16),), jnp.float32),
        "consensus_start": gaussian(key_of[7], (NPOLY, 2, KDIR, P_SIZE), ((CH // NPOLY) ** 0.5), 27.495455, (), jnp.float32),
        "penalty": jnp.clip(jnp.exp(jax.random.uniform(key_of[8], (KDIR,), jnp.float32, math.log(0.3), math.log(3.0))), 0.3, 3.0),
    }


precise = lax.Precision.HIGHEST

def poly_basis(channel_count, degree):
    positions = jnp.arange(channel_count).astype(jnp.float32)
    spread = (2.0 * positions + 1.0) / channel_count - 1.0
    columns = []
    for exponent in range(degree):
        column = spread ** exponent
        for earlier in columns:
            column = column - jnp.sum(column * earlier) * earlier
        column = column / jnp.sqrt(jnp.sum(column * column))
        columns.append(column)
    return jnp.stack(columns, axis=1)

def visibility_products(sky_real, sky_imag, vis_real, vis_imag, weights, first_real, first_imag, second_gain_real, second_imag):
    apparent_real = sky_real * second_gain_real + sky_imag * second_imag
    apparent_imag = sky_imag * second_gain_real - sky_real * second_imag
    predicted_real = first_real * apparent_real - first_imag * apparent_imag
    predicted_imag = first_real * apparent_imag + first_imag * apparent_real
    leftover_real = weights * (vis_real - lax.optimization_barrier(jnp.sum(predicted_real, axis=-3)))
    leftover_imag = weights * (vis_imag - lax.optimization_barrier(jnp.sum(predicted_imag, axis=-3)))
    target_real = jnp.expand_dims(leftover_real, -3) + weights * predicted_real
    target_imag = jnp.expand_dims(leftover_imag, -3) + weights * predicted_imag
    mirror_real = sky_real * first_real - sky_imag * first_imag
    mirror_imag = sky_real * first_imag + sky_imag * first_real
    first_terms = jnp.stack([lax.optimization_barrier(jnp.sum(apparent_real * target_real + apparent_imag * target_imag, axis=-2)), lax.optimization_barrier(jnp.sum(apparent_real * target_imag - apparent_imag * target_real, axis=-2)), lax.optimization_barrier(jnp.sum(weights * (apparent_real * apparent_real + apparent_imag * apparent_imag), axis=-2))])
    second_terms = jnp.stack([lax.optimization_barrier(jnp.sum(mirror_real * target_real + mirror_imag * target_imag, axis=-2)), lax.optimization_barrier(jnp.sum(mirror_imag * target_real - mirror_real * target_imag, axis=-2)), lax.optimization_barrier(jnp.sum(weights * (mirror_real * mirror_real + mirror_imag * mirror_imag), axis=-2))])
    return (first_terms, second_terms)

def gain_update(gain_values, summed, target, dual_values, weight):
    denom = summed[2] + weight
    new_real = (summed[0] + weight * target[0] - dual_values[0]) / denom
    new_imag = (summed[1] + weight * target[1] - dual_values[1]) / denom
    return 0.5 * (gain_values + jnp.stack([new_real, new_imag]))

def station_sum(term_rows, station_ids):
    moved = jnp.moveaxis(term_rows, -1, 0)
    return jnp.moveaxis(jax.ops.segment_sum(moved, station_ids, num_segments=P_SIZE), 0, -1)

def reference(visibilities, sky_model, flag_mask, first_station, second_station, gain_start, dual_start, consensus_start, penalty):
    channel_count = visibilities.shape[1]
    basis_rows = poly_basis(channel_count, NPOLY)
    weight = penalty[:, None]
    target = jnp.einsum('fn,nckp->cfkp', basis_rows, consensus_start, precision=precise)
    flag_weight = flag_mask.astype(jnp.float32)

    def one_channel(channel_items):
        sky_values, vis_values, gain_values, channel_target, dual_values = channel_items
        sky_values = sky_values.astype(jnp.float32)
        for iteration in range(NIT):
            first_gain = jnp.take(gain_values, first_station, axis=2)[:, :, None, :]
            second_gain = jnp.take(gain_values, second_station, axis=2)[:, :, None, :]
            first_terms, second_terms = visibility_products(sky_values[0], sky_values[1], vis_values[0], vis_values[1], flag_weight, first_gain[0], first_gain[1], second_gain[0], second_gain[1])
            summed = station_sum(first_terms, first_station) + station_sum(second_terms, second_station)
            gain_values = gain_update(gain_values, summed, channel_target, dual_values, weight)
        return gain_values
    gain_final = lax.map(one_channel, (jnp.moveaxis(sky_model, 1, 0), jnp.moveaxis(visibilities, 1, 0), jnp.moveaxis(gain_start, 1, 0), jnp.moveaxis(target, 1, 0), jnp.moveaxis(dual_start, 1, 0)))
    gain_final = jnp.moveaxis(gain_final, 0, 1)
    shifted = gain_final + dual_start / weight
    consensus_final = jnp.einsum('fn,cfkp->nckp', basis_rows, shifted, precision=precise)
    fitted = jnp.einsum('fn,nckp->cfkp', basis_rows, consensus_final, precision=precise)
    dual_final = dual_start + weight * (gain_final - fitted)
    return (gain_final, dual_final, consensus_final)
```

```python
import functools

import jax
import jax.numpy as jnp
from jax import lax
from jax.experimental import pallas as pl
from jax.experimental.pallas import tpu as pltpu
from jax.sharding import PartitionSpec as P

NPOLY = 3
NIT = 3
INTERPRET = False
CHUNK = 1024

precise = lax.Precision.HIGHEST
f32 = jnp.float32
bf16 = jnp.bfloat16


def poly_basis(channel_count, degree):
    positions = jnp.arange(channel_count).astype(f32)
    spread = (2.0 * positions + 1.0) / channel_count - 1.0
    columns = []
    for exponent in range(degree):
        column = spread**exponent
        for earlier in columns:
            column = column - jnp.sum(column * earlier) * earlier
        column = column / jnp.sqrt(jnp.sum(column * column))
        columns.append(column)
    return jnp.stack(columns, axis=1)


def two_pieces(x):
    high = x.astype(bf16)
    return high, (x - high.astype(f32)).astype(bf16)


def sums_kernel(first_pass, gain_ref, first_ref, second_ref, sky_ref, vis_ref, seen_ref, *refs):
    if first_pass:
        out_ref, power_ref, *scratch = refs
    else:
        power_ref, out_ref, *scratch = refs
    gain_now_ref, next_ref, wide_ref, cross_ref, sum_ref, terms_ref = scratch
    channels, directions = sky_ref.shape[1:3]
    stations = out_ref.shape[1]
    width = first_ref.shape[1]
    times = sky_ref.shape[3] // 8
    rows = channels * directions
    step = pl.program_id(0)
    last = pl.num_programs(0) - 1
    third = 3 * rows
    iota = lax.broadcasted_iota(jnp.int16, (256, width), 0)

    def scatter(at, lo):
        hots = []
        for ids_ref in (first_ref, second_ref):
            ids = jnp.broadcast_to(ids_ref[pl.ds(at, 1), :].astype(jnp.int16), (256, width))
            hots.append(jnp.where(iota + jnp.int16(lo) == ids, bf16(1), bf16(0)))
        total = lax.dot_general(
            terms_ref[...], jnp.concatenate(hots, axis=1), (((1,), (1,)), ((), ())), preferred_element_type=f32
        )
        out_ref[:, lo : lo + 256] += total[:third] + total[third:]

    def pick_rows(at, f, blocks):
        for k, ids_ref in enumerate((first_ref, second_ref)):
            row = ids_ref[pl.ds(at, 1), :]
            for j in blocks:
                lanes = slice(j * 128, (j + 1) * 128)
                ids = jnp.broadcast_to(row[:, lanes], (8, 128))
                spot = jnp.bitwise_and(ids, 127)
                part = jnp.right_shift(ids, 7)
                for r in (f * directions, rows + f * directions):
                    got = None
                    for b in range(stations // 128):
                        one = jnp.take_along_axis(gain_ref[r : r + 8, b * 128 : (b + 1) * 128], spot, axis=1)
                        got = one if b == 0 else jnp.where(part == b, one, got)
                    next_ref[k, r : r + 8, lanes] = got

    @pl.when(step == 0)
    def _():
        out_ref[...] = jnp.zeros(out_ref.shape, f32)
        terms_ref[...] = jnp.zeros(terms_ref.shape, bf16)
        for f in range(channels):
            pick_rows(0, f, range(8))

    def begin(f):
        at = slice(f * directions, (f + 1) * directions)
        im = slice(rows + f * directions, rows + (f + 1) * directions)
        for j in range(8):
            lanes = slice(j * 128, (j + 1) * 128)
            pr, pi = next_ref[0, at, lanes], next_ref[0, im, lanes]
            qr, qi = next_ref[1, at, lanes], next_ref[1, im, lanes]
            gain_now_ref[0, at, lanes] = pr
            gain_now_ref[0, im, lanes] = pi
            gain_now_ref[1, at, lanes] = qr
            gain_now_ref[1, im, lanes] = qi
            cross_ref[0, f, j * 8 : j * 8 + 8] = pr * qr + pi * qi
            cross_ref[1, f, j * 8 : j * 8 + 8] = pi * qr - pr * qi

    weights = [seen_ref[pl.ds(t, 8, stride=times), :].astype(f32) for t in range(times)]

    def finish(f):
        for j in range(8):
            lanes = slice(j * 128, (j + 1) * 128)
            flat = slice(j * 8, j * 8 + 8)
            pair = [[], [], [], [], [], []]
            for h in (f, f + 1):
                at = slice(h * directions, (h + 1) * directions)
                im = slice(rows + h * directions, rows + (h + 1) * directions)
                pr, pi = gain_now_ref[0, at, lanes], gain_now_ref[0, im, lanes]
                qr, qi = gain_now_ref[1, at, lanes], gain_now_ref[1, im, lanes]
                power = power_ref[h, flat]
                sr = sum_ref[0, h, flat] + cross_ref[0, h, flat] * power
                si = sum_ref[1, h, flat] + cross_ref[1, h, flat] * power
                values = (
                    qr * sr - qi * si,
                    qr * si + qi * sr,
                    power * (qr * qr + qi * qi),
                    pr * sr + pi * si,
                    pi * sr - pr * si,
                    power * (pr * pr + pi * pi),
                )
                for k, v in enumerate(values):
                    pair[k].append(v)
            for k, v in enumerate(pair):
                high, low = two_pieces(jnp.concatenate(v, axis=0))
                to = (k % 3) * rows + f * directions
                there = slice(k // 3 * width + j * 128, k // 3 * width + (j + 1) * 128)
                terms_ref[to : to + 2 * directions, there] = high
                terms_ref[third + to : third + to + 2 * directions, there] = low

    before = jnp.maximum(step - 1, 0)
    after = jnp.minimum(step + 1, last)
    for f in range(channels):
        begin(f)
        for d in range(directions):
            for c in range(2):
                wide_ref[c, f, d] = sky_ref[c, f, d].astype(f32)
        cross = [[cross_ref[c, f, pl.ds(d, 8, stride=8), :] for c in range(2)] for d in range(directions)]
        sums = [None] * directions
        powers = [None] * directions
        for t in range(times):
            if f < 2 and t == 0:
                scatter(before, 256 * f)
            pick_rows(after, f, range(2 * t, 2 * t + 2))
            pick = pl.ds(t, 8, stride=times)
            er = vis_ref[0, f, pick, :]
            ei = vis_ref[1, f, pick, :]
            for d in range(directions):
                gr, gi = cross[d]
                mr = wide_ref[0, f, d, pick, :]
                mi = wide_ref[1, f, d, pick, :]
                er = er - gr * mr + gi * mi
                ei = ei - gr * mi - gi * mr
            er = er * weights[t]
            ei = ei * weights[t]
            for d in range(directions):
                mr = wide_ref[0, f, d, pick, :]
                mi = wide_ref[1, f, d, pick, :]
                sr = mr * er + mi * ei
                si = mr * ei - mi * er
                sums[d] = (sr, si) if t == 0 else (sums[d][0] + sr, sums[d][1] + si)
                if first_pass:
                    power = (mr * mr + mi * mi) * weights[t]
                    powers[d] = power if t == 0 else powers[d] + power
        for d in range(directions):
            spot = pl.ds(d, 8, stride=8)
            sum_ref[0, f, spot, :] = sums[d][0]
            sum_ref[1, f, spot, :] = sums[d][1]
            if first_pass:
                power_ref[f, spot, :] = powers[d]
        if f > 1:
            finish(2 * (f - 2))

    @pl.when(step == last)
    def _():
        for lo in range(0, stations, 256):
            scatter(last, lo)


def station_sums(gain, first_ids, second_ids, sky, vis, seen, power):
    _, channels, directions, total_rows, _ = sky.shape
    grid, width = first_ids.shape
    block_rows = total_rows // grid
    rows = channels * directions
    stations = gain.shape[1]
    first_pass = power is None
    sums_shape = jax.ShapeDtypeStruct((3 * rows, stations), f32)
    sums_spec = pl.BlockSpec((3 * rows, stations), lambda i: (0, 0))
    power_shape = jax.ShapeDtypeStruct((channels, 8 * directions * grid, 128), f32)
    power_spec = pl.BlockSpec((channels, 8 * directions, 128), lambda i: (0, i, 0))
    in_specs = [
        pl.BlockSpec((2 * rows, stations), lambda i: (0, 0)),
        pl.BlockSpec((grid, width), lambda i: (0, 0)),
        pl.BlockSpec((grid, width), lambda i: (0, 0)),
        pl.BlockSpec((2, channels, directions, block_rows, 128), lambda i: (0, 0, 0, i, 0)),
        pl.BlockSpec((2, channels, block_rows, 128), lambda i: (0, 0, i, 0)),
        pl.BlockSpec((block_rows, 128), lambda i: (i, 0)),
    ]
    args = [gain, first_ids, second_ids, sky, vis, seen]
    if not first_pass:
        in_specs.append(power_spec)
        args.append(power)
    out = pl.pallas_call(
        functools.partial(sums_kernel, first_pass),
        out_shape=(sums_shape, power_shape) if first_pass else sums_shape,
        grid=(grid,),
        in_specs=in_specs,
        out_specs=(sums_spec, power_spec) if first_pass else sums_spec,
        scratch_shapes=[
            pltpu.VMEM((2, 2 * rows, width), f32),
            pltpu.VMEM((2, 2 * rows, width), f32),
            pltpu.VMEM((2, channels, directions, block_rows, 128), f32),
            pltpu.VMEM((2, channels, 8 * directions, 128), f32),
            pltpu.VMEM((2, channels, 8 * directions, 128), f32),
            pltpu.VMEM((6 * rows, 2 * width), bf16),
        ],
        compiler_params=pltpu.CompilerParams(dimension_semantics=("arbitrary",), vmem_limit_bytes=48 << 20),
        interpret=INTERPRET,
    )(*args)
    return out if first_pass else (out, power)


def tile_rows(x):
    *lead, times, antenna_pairs = x.shape
    x = x.reshape(*lead, times, antenna_pairs // 128, 128)
    return jnp.swapaxes(x, -3, -2).reshape(*lead, antenna_pairs // 128 * times, 128)


def sum_over_bl(x):
    if lax.axis_size("bl") == 1:
        return x
    flips = [lambda y, x: (y, x ^ 1), lambda y, x: (y, 3 - x), lambda y, x: (y ^ 1, x), lambda y, x: (3 - y, x)]
    orders = [(0, 1, 2, 3), (2, 3, 0, 1)]
    for step in range(4):
        pairs = []
        for freq in range(16):
            flip = flips[orders[freq % 2][step]]
            for y in range(4):
                for x_at in range(4):
                    ty, tx = flip(y, x_at)
                    pairs.append((freq * 16 + y * 4 + x_at, freq * 16 + ty * 4 + tx))
        x = x + lax.ppermute(x, ("freq", "bl"), pairs)
    return x


def sum_over_freq(x):
    if lax.axis_size("freq") == 1:
        return x
    half = x.shape[0] // 2
    core = lax.axis_index("freq") % 2
    swap = [(i, i ^ 1) for i in range(16)]
    mine = lax.dynamic_slice_in_dim(x, core * half, half, 0)
    other = lax.dynamic_slice_in_dim(x, (1 - core) * half, half, 0)
    mine = mine + lax.ppermute(other, "freq", swap)
    for bit in (2, 4, 8):
        mine = mine + lax.ppermute(mine, "freq", [(i, i ^ bit) for i in range(16)])
    other = lax.ppermute(mine, "freq", swap)
    return jnp.where(core == 0, jnp.concatenate([mine, other]), jnp.concatenate([other, mine]))


def per_device(
    visibilities, sky_model, flag_mask, first_station, second_station, gain_start, dual_start, consensus_start, penalty
):
    local_channels = visibilities.shape[1]
    directions = gain_start.shape[2]
    stations = gain_start.shape[3]
    rows = local_channels * directions
    channel_count = local_channels * lax.axis_size("freq")
    basis_rows = poly_basis(channel_count, NPOLY)
    local_rows = lax.dynamic_slice_in_dim(basis_rows, lax.axis_index("freq") * local_channels, local_channels, 0)
    weight = penalty[:, None]
    target = jnp.einsum("fn,nckp->cfkp", local_rows, consensus_start, precision=precise)
    pull = weight * target - dual_start
    sky = tile_rows(sky_model)
    vis = tile_rows(visibilities)
    seen = tile_rows(flag_mask)
    first_ids = first_station.reshape(-1, CHUNK)
    second_ids = second_station.reshape(-1, CHUNK)
    gain_now = gain_start
    power = None
    for _ in range(NIT):
        table = gain_now.reshape(2 * rows, stations)
        partial, power = station_sums(table, first_ids, second_ids, sky, vis, seen, power)
        summed = sum_over_bl(partial).reshape(3, local_channels, directions, stations)
        gain_now = 0.5 * (gain_now + (summed[:2] + pull) / (summed[2] + weight))
    shifted = gain_now + dual_start / weight
    local_part = jnp.einsum("fn,cfkp->nckp", local_rows, shifted, precision=precise)
    consensus_final = sum_over_freq(local_part.reshape(2 * NPOLY * directions, stations)).reshape(local_part.shape)
    fitted = jnp.einsum("fn,nckp->cfkp", local_rows, consensus_final, precision=precise)
    dual_final = dual_start + weight * (gain_now - fitted)
    return (gain_now, dual_final, consensus_final)


def solution(mesh):
    in_specs = (
        P(None, "freq", None, "bl"),
        P(None, "freq", None, None, "bl"),
        P(None, "bl"),
        P("bl"),
        P("bl"),
        P(None, "freq", None, None),
        P(None, "freq", None, None),
        P(),
        P(),
    )
    out_specs = (P(None, "freq", None, None), P(None, "freq", None, None), P())
    return jax.shard_map(per_device, mesh=mesh, in_specs=in_specs, out_specs=out_specs, check_vma=False)
```

```python
import functools

import jax
import jax.numpy as jnp
import numpy as np
from jax import lax
from jax.experimental import pallas as pl
from jax.experimental.pallas import tpu as pltpu
from jax.sharding import PartitionSpec as P

NPOLY = 3
NIT = 3
INTERPRET = False

precise = lax.Precision.HIGHEST
f32 = jnp.float32
bf16 = jnp.bfloat16


def poly_basis(channel_count, degree):
    positions = np.arange(channel_count, dtype=np.float32)
    spread = (np.float32(2) * positions + np.float32(1)) / np.float32(channel_count) - np.float32(1)
    columns = []
    for exponent in range(degree):
        column = spread**exponent
        for earlier in columns:
            column = column - np.sum(column * earlier) * earlier
        columns.append((column / np.sqrt(np.sum(column * column))).astype(np.float32))
    return jnp.asarray(np.stack(columns, axis=1))


def two_pieces(x):
    high = x.astype(bf16)
    return high, (x - high.astype(f32)).astype(bf16)


def sums_kernel(first_pass, gain_ref, first_ref, second_ref, sky_ref, vis_ref, seen_ref, *refs):
    if first_pass:
        out_ref, power_ref, *scratch = refs
    else:
        power_ref, out_ref, *scratch = refs
    gain_now_ref, next_ref, wide_ref, cross_ref, sum_ref, terms_ref = scratch
    channels, directions = sky_ref.shape[1:3]
    stations = out_ref.shape[1]
    width = 8 * 128
    times = sky_ref.shape[3] // 8
    rows = channels * directions
    step = pl.program_id(0)
    last = pl.num_programs(0) - 1
    third = 3 * rows
    iota = lax.broadcasted_iota(jnp.int16, (256, 128), 0)

    def scatter(at, lo):
        hots = []
        for ids_ref in (first_ref, second_ref):
            for j in range(8):
                ids = jnp.broadcast_to(ids_ref[pl.ds(at * 8 + j, 1), :].astype(jnp.int16), (256, 128))
                hots.append(jnp.where(iota + jnp.int16(lo) == ids, bf16(1), bf16(0)))
        total = lax.dot_general(
            terms_ref[...], jnp.concatenate(hots, axis=1), (((1,), (1,)), ((), ())), preferred_element_type=f32
        )
        out_ref[:, lo : lo + 256] += total[:third] + total[third:]

    def pick_rows(at, n):
        k, j = n // 8, n % 8
        ids = jnp.broadcast_to((first_ref, second_ref)[k][pl.ds(at * 8 + j, 1), :], (8, 128))
        spot = jnp.bitwise_and(ids, 127)
        part = jnp.right_shift(ids, 7)
        same = [part == b for b in range(1, stations // 128)]
        for r in range(0, 2 * rows, 8):
            got = None
            for b in range(stations // 128):
                one = jnp.take_along_axis(gain_ref[r : r + 8, b * 128 : (b + 1) * 128], spot, axis=1)
                got = one if b == 0 else jnp.where(same[b - 1], one, got)
            next_ref[k, r : r + 8, j * 128 : (j + 1) * 128] = got

    @pl.when(step == 0)
    def _():
        out_ref[...] = jnp.zeros(out_ref.shape, f32)
        terms_ref[...] = jnp.zeros(terms_ref.shape, bf16)
        for n in range(16):
            pick_rows(0, n)

    def begin(f):
        at = slice(f * directions, (f + 1) * directions)
        im = slice(rows + f * directions, rows + (f + 1) * directions)
        for j in range(8):
            lanes = slice(j * 128, (j + 1) * 128)
            pr, pi = next_ref[0, at, lanes], next_ref[0, im, lanes]
            qr, qi = next_ref[1, at, lanes], next_ref[1, im, lanes]
            gain_now_ref[0, at, lanes] = pr
            gain_now_ref[0, im, lanes] = pi
            gain_now_ref[1, at, lanes] = qr
            gain_now_ref[1, im, lanes] = qi
            cross_ref[0, f, j * 8 : j * 8 + 8] = pr * qr + pi * qi
            cross_ref[1, f, j * 8 : j * 8 + 8] = pi * qr - pr * qi

    weights = [seen_ref[pl.ds(t, 8, stride=times), :].astype(f32) for t in range(times)]

    def finish(f):
        at = slice(f * directions, (f + 1) * directions)
        im = slice(rows + f * directions, rows + (f + 1) * directions)
        for j in range(8):
            lanes = slice(j * 128, (j + 1) * 128)
            flat = slice(j * 8, j * 8 + 8)
            pr, pi = gain_now_ref[0, at, lanes], gain_now_ref[0, im, lanes]
            qr, qi = gain_now_ref[1, at, lanes], gain_now_ref[1, im, lanes]
            power = power_ref[f, flat]
            sr = sum_ref[0, f, flat] + cross_ref[0, f, flat] * power
            si = sum_ref[1, f, flat] + cross_ref[1, f, flat] * power
            values = (
                qr * sr - qi * si,
                qr * si + qi * sr,
                power * (qr * qr + qi * qi),
                pr * sr + pi * si,
                pi * sr - pr * si,
                power * (pr * pr + pi * pi),
            )
            for k, v in enumerate(values):
                high, low = two_pieces(v)
                to = (k % 3) * rows + f * directions
                there = slice(k // 3 * width + j * 128, k // 3 * width + (j + 1) * 128)
                terms_ref[to : to + directions, there] = high
                terms_ref[third + to : third + to + directions, there] = low

    before = jnp.maximum(step - 1, 0)
    after = jnp.minimum(step + 1, last)
    for f in range(channels):
        begin(f)
    for f in range(channels):
        for d in range(directions):
            for c in range(2):
                wide_ref[c, f, d] = sky_ref[c, f, d].astype(f32)
        cross = [[cross_ref[c, f, pl.ds(d, 8, stride=8), :] for c in range(2)] for d in range(directions)]
        sums = [None] * directions
        powers = [None] * directions
        for t in range(times):
            if f < 2 and t == 0:
                scatter(before, 256 * f)
            pick_rows(after, f * times + t)
            pick = pl.ds(t, 8, stride=times)
            er = vis_ref[0, f, pick, :]
            ei = vis_ref[1, f, pick, :]
            for d in range(directions):
                gr, gi = cross[d]
                mr = wide_ref[0, f, d, pick, :]
                mi = wide_ref[1, f, d, pick, :]
                er = er - gr * mr + gi * mi
                ei = ei - gr * mi - gi * mr
            er = er * weights[t]
            ei = ei * weights[t]
            for d in range(directions):
                mr = wide_ref[0, f, d, pick, :]
                mi = wide_ref[1, f, d, pick, :]
                sr = mr * er + mi * ei
                si = mr * ei - mi * er
                sums[d] = (sr, si) if t == 0 else (sums[d][0] + sr, sums[d][1] + si)
                if first_pass:
                    power = (mr * mr + mi * mi) * weights[t]
                    powers[d] = power if t == 0 else powers[d] + power
        for d in range(directions):
            spot = pl.ds(d, 8, stride=8)
            sum_ref[0, f, spot, :] = sums[d][0]
            sum_ref[1, f, spot, :] = sums[d][1]
            if first_pass:
                power_ref[f, spot, :] = powers[d]
        if f > 1:
            finish(2 * (f - 2))
            finish(2 * (f - 2) + 1)

    @pl.when(step == last)
    def _():
        for lo in range(0, stations, 256):
            scatter(last, lo)


def station_sums(gain, first_ids, second_ids, sky, vis, seen, power):
    _, channels, directions, total_rows, _ = sky.shape
    width = 8 * 128
    grid = first_ids.shape[0] // 8
    block_rows = total_rows // grid
    rows = channels * directions
    stations = gain.shape[1]
    first_pass = power is None
    sums_shape = jax.ShapeDtypeStruct((3 * rows, stations), f32)
    sums_spec = pl.BlockSpec((3 * rows, stations), lambda i: (0, 0))
    power_shape = jax.ShapeDtypeStruct((channels, 8 * directions * grid, 128), f32)
    power_spec = pl.BlockSpec((channels, 8 * directions, 128), lambda i: (0, i, 0))
    in_specs = [
        pl.BlockSpec((2 * rows, stations), lambda i: (0, 0)),
        pl.BlockSpec((8 * grid, 128), lambda i: (0, 0)),
        pl.BlockSpec((8 * grid, 128), lambda i: (0, 0)),
        pl.BlockSpec((2, channels, directions, block_rows, 128), lambda i: (0, 0, 0, i, 0)),
        pl.BlockSpec((2, channels, block_rows, 128), lambda i: (0, 0, i, 0)),
        pl.BlockSpec((block_rows, 128), lambda i: (i, 0)),
    ]
    args = [gain, first_ids, second_ids, sky, vis, seen]
    if not first_pass:
        in_specs.append(power_spec)
        args.append(power)
    out = pl.pallas_call(
        functools.partial(sums_kernel, first_pass),
        out_shape=(sums_shape, power_shape) if first_pass else sums_shape,
        grid=(grid,),
        in_specs=in_specs,
        out_specs=(sums_spec, power_spec) if first_pass else sums_spec,
        scratch_shapes=[
            pltpu.VMEM((2, 2 * rows, width), f32),
            pltpu.VMEM((2, 2 * rows, width), f32),
            pltpu.VMEM((2, channels, directions, block_rows, 128), f32),
            pltpu.VMEM((2, channels, 8 * directions, 128), f32),
            pltpu.VMEM((2, channels, 8 * directions, 128), f32),
            pltpu.VMEM((6 * rows, 2 * width), bf16),
        ],
        compiler_params=pltpu.CompilerParams(dimension_semantics=("arbitrary",), vmem_limit_bytes=48 << 20),
        interpret=INTERPRET,
    )(*args)
    return out if first_pass else (out, power)


def in_hbm(x):
    return x if INTERPRET else pltpu.with_memory_space_constraint(x, pltpu.HBM)


def tile_rows(x):
    *lead, times, antenna_pairs = x.shape
    x = x.reshape(*lead, times, antenna_pairs // 128, 128)
    return jnp.swapaxes(x, -3, -2).reshape(*lead, antenna_pairs // 128 * times, 128)


def sum_over_bl(x):
    if lax.axis_size("bl") == 1:
        return x
    flips = [lambda y, x: (y, x ^ 1), lambda y, x: (y, 3 - x), lambda y, x: (y ^ 1, x), lambda y, x: (3 - y, x)]
    orders = [(0, 1, 2, 3), (2, 3, 0, 1)]
    for step in range(4):
        pairs = []
        for freq in range(16):
            flip = flips[orders[freq % 2][step]]
            for y in range(4):
                for x_at in range(4):
                    ty, tx = flip(y, x_at)
                    pairs.append((freq * 16 + y * 4 + x_at, freq * 16 + ty * 4 + tx))
        x = x + lax.ppermute(x, ("freq", "bl"), pairs)
    return x


def sum_over_freq(x):
    if lax.axis_size("freq") == 1:
        return x
    half = x.shape[0] // 2
    core = lax.axis_index("freq") % 2
    swap = [(i, i ^ 1) for i in range(16)]
    mine = lax.dynamic_slice_in_dim(x, core * half, half, 0)
    other = lax.dynamic_slice_in_dim(x, (1 - core) * half, half, 0)
    mine = mine + lax.ppermute(other, "freq", swap)
    mine = mine + lax.ppermute(mine, "freq", [(i, i ^ 2) for i in range(16)])
    far, up, down = [lax.ppermute(mine, "freq", [(i, (i + by) % 16) for i in range(16)]) for by in (8, 4, 12)]
    mine = (mine + far) + (up + down)
    other = lax.ppermute(mine, "freq", swap)
    return jnp.where(core == 0, jnp.concatenate([mine, other]), jnp.concatenate([other, mine]))


def per_device(
    visibilities, sky_model, flag_mask, first_station, second_station, gain_start, dual_start, consensus_start, penalty
):
    local_channels = visibilities.shape[1]
    directions = gain_start.shape[2]
    stations = gain_start.shape[3]
    rows = local_channels * directions
    channel_count = local_channels * lax.axis_size("freq")
    basis_rows = poly_basis(channel_count, NPOLY)
    local_rows = lax.dynamic_slice_in_dim(basis_rows, lax.axis_index("freq") * local_channels, local_channels, 0)
    weight = penalty[:, None]
    target = jnp.einsum("fn,nckp->cfkp", local_rows, consensus_start, precision=precise)
    pull = weight * target - dual_start
    sky = in_hbm(tile_rows(sky_model))
    vis = in_hbm(tile_rows(visibilities))
    seen = in_hbm(tile_rows(flag_mask))
    first_ids = in_hbm(first_station.reshape(-1, 128))
    second_ids = in_hbm(second_station.reshape(-1, 128))
    gain_now = gain_start
    power = None
    for turn in range(NIT):
        table = gain_now.reshape(2 * rows, stations)
        if turn == 0:
            table = in_hbm(table)
        partial, power = station_sums(table, first_ids, second_ids, sky, vis, seen, power)
        summed = sum_over_bl(partial).reshape(3, local_channels, directions, stations)
        gain_now = 0.5 * (gain_now + (summed[:2] + pull) / (summed[2] + weight))
    shifted = gain_now + dual_start / weight
    local_part = jnp.sum(local_rows.T[:, None, :, None, None] * shifted[None], axis=2)
    consensus_final = sum_over_freq(local_part.reshape(2 * NPOLY * directions, stations)).reshape(local_part.shape)
    fitted = sum(local_rows[None, :, n, None, None] * consensus_final[n][:, None] for n in range(NPOLY))
    dual_final = dual_start + weight * (gain_now - fitted)
    return (gain_now, dual_final, consensus_final)


def solution(mesh):
    in_specs = (
        P(None, "freq", None, "bl"),
        P(None, "freq", None, None, "bl"),
        P(None, "bl"),
        P("bl"),
        P("bl"),
        P(None, "freq", None, None),
        P(None, "freq", None, None),
        P(),
        P(),
    )
    out_specs = (P(None, "freq", None, None), P(None, "freq", None, None), P())
    return jax.shard_map(per_device, mesh=mesh, in_specs=in_specs, out_specs=out_specs, check_vma=False)
```

```python
import functools

import jax
import jax.numpy as jnp
import numpy as np
from jax import lax
from jax.experimental import pallas as pl
from jax.experimental.pallas import tpu as pltpu
from jax.sharding import PartitionSpec as P

NPOLY = 3
NIT = 3
INTERPRET = False

precise = lax.Precision.HIGHEST
f32 = jnp.float32
bf16 = jnp.bfloat16


def poly_basis(channel_count, degree):
    positions = np.arange(channel_count, dtype=np.float32)
    spread = (np.float32(2) * positions + np.float32(1)) / np.float32(channel_count) - np.float32(1)
    columns = []
    for exponent in range(degree):
        column = spread**exponent
        for earlier in columns:
            column = column - np.sum(column * earlier) * earlier
        columns.append((column / np.sqrt(np.sum(column * column))).astype(np.float32))
    return jnp.asarray(np.stack(columns, axis=1))


def two_pieces(x):
    high = x.astype(bf16)
    return high, (x - high.astype(f32)).astype(bf16)


def sums_kernel(first_pass, gain_ref, first_ref, second_ref, sky_ref, vis_ref, seen_ref, *refs):
    if first_pass:
        out_ref, power_ref, *scratch = refs
    else:
        power_ref, out_ref, *scratch = refs
    gain_now_ref, next_ref, wide_ref, cross_ref, sum_ref, terms_ref = scratch
    channels, directions = sky_ref.shape[1:3]
    stations = out_ref.shape[1]
    width = 8 * 128
    times = sky_ref.shape[3] // 8
    rows = channels * directions
    step = pl.program_id(0)
    last = pl.num_programs(0) - 1
    third = 3 * rows
    iota = lax.broadcasted_iota(jnp.int16, (256, 128), 0)

    def scatter(at, lo):
        hots = []
        for ids_ref in (first_ref, second_ref):
            for j in range(8):
                ids = jnp.broadcast_to(ids_ref[pl.ds(at * 8 + j, 1), :].astype(jnp.int16), (256, 128))
                hots.append(jnp.where(iota + jnp.int16(lo) == ids, bf16(1), bf16(0)))
        total = lax.dot_general(
            terms_ref[...], jnp.concatenate(hots, axis=1), (((1,), (1,)), ((), ())), preferred_element_type=f32
        )
        out_ref[:, lo : lo + 256] += total[:third] + total[third:]

    def pick_rows(at, n):
        k, j = n // 8, n % 8
        ids = jnp.broadcast_to((first_ref, second_ref)[k][pl.ds(at * 8 + j, 1), :], (8, 128))
        spot = jnp.bitwise_and(ids, 127)
        part = jnp.right_shift(ids, 7)
        same = [part == b for b in range(1, stations // 128)]
        for r in range(0, 2 * rows, 8):
            got = None
            for b in range(stations // 128):
                one = jnp.take_along_axis(gain_ref[r : r + 8, b * 128 : (b + 1) * 128], spot, axis=1)
                got = one if b == 0 else jnp.where(same[b - 1], one, got)
            next_ref[k, r : r + 8, j * 128 : (j + 1) * 128] = got

    @pl.when(step == 0)
    def _():
        out_ref[...] = jnp.zeros(out_ref.shape, f32)
        terms_ref[...] = jnp.zeros(terms_ref.shape, bf16)
        for n in range(16):
            pick_rows(0, n)

    def begin(f):
        at = slice(f * directions, (f + 1) * directions)
        im = slice(rows + f * directions, rows + (f + 1) * directions)
        for j in range(8):
            lanes = slice(j * 128, (j + 1) * 128)
            pr, pi = next_ref[0, at, lanes], next_ref[0, im, lanes]
            qr, qi = next_ref[1, at, lanes], next_ref[1, im, lanes]
            gain_now_ref[0, at, lanes] = pr
            gain_now_ref[0, im, lanes] = pi
            gain_now_ref[1, at, lanes] = qr
            gain_now_ref[1, im, lanes] = qi
            cross_ref[0, f, j * 8 : j * 8 + 8] = pr * qr + pi * qi
            cross_ref[1, f, j * 8 : j * 8 + 8] = pi * qr - pr * qi

    weights = [seen_ref[pl.ds(t, 8, stride=times), :].astype(f32) for t in range(times)]

    def finish(f):
        at = slice(f * directions, (f + 1) * directions)
        im = slice(rows + f * directions, rows + (f + 1) * directions)
        for j in range(8):
            lanes = slice(j * 128, (j + 1) * 128)
            flat = slice(j * 8, j * 8 + 8)
            pr, pi = gain_now_ref[0, at, lanes], gain_now_ref[0, im, lanes]
            qr, qi = gain_now_ref[1, at, lanes], gain_now_ref[1, im, lanes]
            power = power_ref[f, flat]
            sr = sum_ref[0, f, flat] + cross_ref[0, f, flat] * power
            si = sum_ref[1, f, flat] + cross_ref[1, f, flat] * power
            values = (
                qr * sr - qi * si,
                qr * si + qi * sr,
                power * (qr * qr + qi * qi),
                pr * sr + pi * si,
                pi * sr - pr * si,
                power * (pr * pr + pi * pi),
            )
            for k, v in enumerate(values):
                high, low = two_pieces(v)
                to = (k % 3) * rows + f * directions
                there = slice(k // 3 * width + j * 128, k // 3 * width + (j + 1) * 128)
                terms_ref[to : to + directions, there] = high
                terms_ref[third + to : third + to + directions, there] = low

    before = jnp.maximum(step - 1, 0)
    after = jnp.minimum(step + 1, last)
    for f in range(channels):
        begin(f)
    for f in range(channels):
        for d in range(directions):
            for c in range(2):
                wide_ref[c, f, d] = sky_ref[c, f, d].astype(f32)
        cross = [[cross_ref[c, f, pl.ds(d, 8, stride=8), :] for c in range(2)] for d in range(directions)]
        sums = [None] * directions
        powers = [None] * directions
        for t in range(times):
            if f in (1, 2) and t == 0:
                scatter(before, 256 * (f - 1))
            if f == 0:
                for n in range(4):
                    pick_rows(after, 4 * t + n)
            pick = pl.ds(t, 8, stride=times)
            er = vis_ref[0, f, pick, :]
            ei = vis_ref[1, f, pick, :]
            for d in range(directions):
                gr, gi = cross[d]
                mr = wide_ref[0, f, d, pick, :]
                mi = wide_ref[1, f, d, pick, :]
                er = er - gr * mr + gi * mi
                ei = ei - gr * mi - gi * mr
            er = er * weights[t]
            ei = ei * weights[t]
            for d in range(directions):
                mr = wide_ref[0, f, d, pick, :]
                mi = wide_ref[1, f, d, pick, :]
                sr = mr * er + mi * ei
                si = mr * ei - mi * er
                sums[d] = (sr, si) if t == 0 else (sums[d][0] + sr, sums[d][1] + si)
                if first_pass:
                    power = (mr * mr + mi * mi) * weights[t]
                    powers[d] = power if t == 0 else powers[d] + power
        for d in range(directions):
            spot = pl.ds(d, 8, stride=8)
            sum_ref[0, f, spot, :] = sums[d][0]
            sum_ref[1, f, spot, :] = sums[d][1]
            if first_pass:
                power_ref[f, spot, :] = powers[d]
    for f in range(channels):
        finish(f)

    @pl.when(step == last)
    def _():
        for lo in range(0, stations, 256):
            scatter(last, lo)


def station_sums(gain, first_ids, second_ids, sky, vis, seen, power):
    _, channels, directions, total_rows, _ = sky.shape
    width = 8 * 128
    grid = first_ids.shape[0] // 8
    block_rows = total_rows // grid
    rows = channels * directions
    stations = gain.shape[1]
    first_pass = power is None
    sums_shape = jax.ShapeDtypeStruct((3 * rows, stations), f32)
    sums_spec = pl.BlockSpec((3 * rows, stations), lambda i: (0, 0))
    power_shape = jax.ShapeDtypeStruct((channels, 8 * directions * grid, 128), f32)
    power_spec = pl.BlockSpec((channels, 8 * directions, 128), lambda i: (0, i, 0))
    in_specs = [
        pl.BlockSpec((2 * rows, stations), lambda i: (0, 0)),
        pl.BlockSpec((8 * grid, 128), lambda i: (0, 0)),
        pl.BlockSpec((8 * grid, 128), lambda i: (0, 0)),
        pl.BlockSpec((2, channels, directions, block_rows, 128), lambda i: (0, 0, 0, i, 0)),
        pl.BlockSpec((2, channels, block_rows, 128), lambda i: (0, 0, i, 0)),
        pl.BlockSpec((block_rows, 128), lambda i: (i, 0)),
    ]
    args = [gain, first_ids, second_ids, sky, vis, seen]
    if not first_pass:
        in_specs.append(power_spec)
        args.append(power)
    out = pl.pallas_call(
        functools.partial(sums_kernel, first_pass),
        out_shape=(sums_shape, power_shape) if first_pass else sums_shape,
        grid=(grid,),
        in_specs=in_specs,
        out_specs=(sums_spec, power_spec) if first_pass else sums_spec,
        scratch_shapes=[
            pltpu.VMEM((2, 2 * rows, width), f32),
            pltpu.VMEM((2, 2 * rows, width), f32),
            pltpu.VMEM((2, channels, directions, block_rows, 128), f32),
            pltpu.VMEM((2, channels, 8 * directions, 128), f32),
            pltpu.VMEM((2, channels, 8 * directions, 128), f32),
            pltpu.VMEM((6 * rows, 2 * width), bf16),
        ],
        compiler_params=pltpu.CompilerParams(dimension_semantics=("arbitrary",), vmem_limit_bytes=48 << 20),
        interpret=INTERPRET,
    )(*args)
    return out if first_pass else (out, power)


def in_hbm(x):
    return x if INTERPRET else pltpu.with_memory_space_constraint(x, pltpu.HBM)


def tile_rows(x):
    *lead, times, antenna_pairs = x.shape
    x = x.reshape(*lead, times, antenna_pairs // 128, 128)
    return jnp.swapaxes(x, -3, -2).reshape(*lead, antenna_pairs // 128 * times, 128)


def sum_over_bl(x):
    if lax.axis_size("bl") == 1:
        return x
    flips = [lambda y, x: (y, x ^ 1), lambda y, x: (y, 3 - x), lambda y, x: (y ^ 1, x), lambda y, x: (3 - y, x)]
    orders = [(0, 1, 2, 3), (2, 3, 0, 1)]
    for step in range(4):
        pairs = []
        for freq in range(16):
            flip = flips[orders[freq % 2][step]]
            for y in range(4):
                for x_at in range(4):
                    ty, tx = flip(y, x_at)
                    pairs.append((freq * 16 + y * 4 + x_at, freq * 16 + ty * 4 + tx))
        x = x + lax.ppermute(x, ("freq", "bl"), pairs)
    return x


def sum_over_freq(x):
    if lax.axis_size("freq") == 1:
        return x
    half = x.shape[0] // 2
    core = lax.axis_index("freq") % 2
    swap = [(i, i ^ 1) for i in range(16)]
    mine = lax.dynamic_slice_in_dim(x, core * half, half, 0)
    other = lax.dynamic_slice_in_dim(x, (1 - core) * half, half, 0)
    mine = mine + lax.ppermute(other, "freq", swap)
    mine = mine + lax.ppermute(mine, "freq", [(i, i ^ 2) for i in range(16)])
    far, up, down = [lax.ppermute(mine, "freq", [(i, (i + by) % 16) for i in range(16)]) for by in (8, 4, 12)]
    mine = (mine + far) + (up + down)
    other = lax.ppermute(mine, "freq", swap)
    return jnp.where(core == 0, jnp.concatenate([mine, other]), jnp.concatenate([other, mine]))


def per_device(
    visibilities, sky_model, flag_mask, first_station, second_station, gain_start, dual_start, consensus_start, penalty
):
    local_channels = visibilities.shape[1]
    directions = gain_start.shape[2]
    stations = gain_start.shape[3]
    rows = local_channels * directions
    channel_count = local_channels * lax.axis_size("freq")
    basis_rows = poly_basis(channel_count, NPOLY)
    local_rows = lax.dynamic_slice_in_dim(basis_rows, lax.axis_index("freq") * local_channels, local_channels, 0)
    weight = penalty[:, None]
    target = jnp.einsum("fn,nckp->cfkp", local_rows, consensus_start, precision=precise)
    pull = weight * target - dual_start
    sky = in_hbm(tile_rows(sky_model))
    vis = in_hbm(tile_rows(visibilities))
    seen = in_hbm(tile_rows(flag_mask))
    first_ids = in_hbm(first_station.reshape(-1, 128))
    second_ids = in_hbm(second_station.reshape(-1, 128))
    gain_now = gain_start
    power = None
    for turn in range(NIT):
        table = gain_now.reshape(2 * rows, stations)
        if turn == 0:
            table = in_hbm(table)
        partial, power = station_sums(table, first_ids, second_ids, sky, vis, seen, power)
        summed = sum_over_bl(partial).reshape(3, local_channels, directions, stations)
        gain_now = 0.5 * (gain_now + (summed[:2] + pull) / (summed[2] + weight))
    shifted = gain_now + dual_start / weight
    local_part = jnp.sum(local_rows.T[:, None, :, None, None] * shifted[None], axis=2)
    consensus_final = sum_over_freq(local_part.reshape(2 * NPOLY * directions, stations)).reshape(local_part.shape)
    fitted = sum(local_rows[None, :, n, None, None] * consensus_final[n][:, None] for n in range(NPOLY))
    dual_final = dual_start + weight * (gain_now - fitted)
    return (gain_now, dual_final, consensus_final)


def solution(mesh):
    in_specs = (
        P(None, "freq", None, "bl"),
        P(None, "freq", None, None, "bl"),
        P(None, "bl"),
        P("bl"),
        P("bl"),
        P(None, "freq", None, None),
        P(None, "freq", None, None),
        P(),
        P(),
    )
    out_specs = (P(None, "freq", None, None), P(None, "freq", None, None), P())
    return jax.shard_map(per_device, mesh=mesh, in_specs=in_specs, out_specs=out_specs, check_vma=False)
```
